32 devices in a mesh: fsdp: 16 (over z, x, core), dp: 2 (over y).
Axes of the slice: x: 2, y: 2, z: 4, core: 2. Of those that a mesh axis runs over, the one named last changes fastest.
Arguments:
- inputs: bfloat16 [6144, 4096], P(('fsdp', 'dp')), may hold values from -6 to 6
- grad_out: bfloat16 [6144, 14336], P(('fsdp', 'dp')), may hold values from -0.009765625 to 0.009765625
- projection: bfloat16 [4096, 128], P('fsdp'), may hold values from -0.375 to 0.375
- moment: float32 [14336, 128], P('fsdp'), may hold values from -1.5 to 1.5
- second: float32 [14336, 128], P('fsdp'), may hold values from 0.0001 to 0.001
Outputs:
- update: bfloat16 [4096, 14336], P('fsdp')
- new_moment: float32 [14336, 128], P('fsdp')
- new_second: float32 [14336, 128], P('fsdp')
The draws below stay inside these ranges and needn't reach their ends.
All inputs are finite; a program needn't handle non-finite values.
Results may differ from the reference program's by a relative error of at most 0.0051.
Values may be sent and summed in bfloat16 or wider, within the bound.
No kernel may reach another device: no remote copies, remote signals or barrier semaphores. Data moves between devices by JAX's collectives and lax.ppermute only.
A program may use at most 64 MiB of HBM per device.

```python
import math
import jax
import jax.numpy as jnp
from jax import lax

D = 4096
FF = 14336
RANK = 128
STEP = 10
TOKENS = 6144


def strengthened(values, rng, source, target, blocks, factor):
    owner, partner = [(jnp.arange(values.shape[position]) // (values.shape[position] // blocks)).reshape([-1 if axis == position else 1 for axis in range(values.ndim)]) for position in (source, target)]
    chosen = jax.random.permutation(rng, blocks)[partner]
    strong = (owner == chosen) | (owner == (partner + blocks // 2) % blocks)
    return jnp.where(strong, factor * values, values)


def block_scale(stream_key, dims, shards, smallest, top_value):
    def one(position, parts):
        draws = jax.random.uniform(jax.random.fold_in(jax.random.fold_in(stream_key, 6), position), (parts,), jnp.float32, smallest / len(shards), top_value / len(shards))
        return jnp.repeat(jnp.exp(draws), dims[position] // parts).reshape((-1,) + (1,) * (len(dims) - position - 1))

    gain = one(*shards[0])
    for cut in shards[1:]:
        gain = gain * one(*cut)
    return gain


def scatter_about(rng, shape, width, reach, cuts=(), held_as=jnp.bfloat16):
    result = jax.random.normal(rng, shape, jnp.float32) * width
    if len(cuts) > 0:
        result = block_scale(rng, shape, cuts, -0.22, 0.18) * result
    return jnp.clip(result, min=-reach, max=reach).astype(held_as)


def gaussian_with(stream_key, shape, spread, bound, split, heavy, dtype=jnp.bfloat16):
    entries = spread * jax.random.normal(stream_key, shape, jnp.float32)
    if split:
        entries = entries * block_scale(stream_key, shape, split, -0.22, 0.18)
    return jnp.clip(strengthened(entries, jax.random.fold_in(stream_key, 3), *heavy), -bound, bound).astype(dtype)


def setup_inputs(seed: int = 0) -> dict:
    splits = jax.random.split(jax.random.key(seed), 6)
    inputs = scatter_about(splits[0], (TOKENS, D), 1.0, 6.0, ((0, 32),))
    grad_out = gaussian_with(splits[1], (TOKENS, FF), (TOKENS * 256) ** -0.5, 0.009765625, ((0, 32),), (0, 1, 32, 2.75))
    projection = scatter_about(splits[2], (D, RANK), (D // 16) ** -0.5, 0.375, ((0, 16),))
    moment = scatter_about(splits[3], (FF, RANK), 0.25, 1.5, ((0, 16),), jnp.float32)
    second = jnp.clip(jnp.exp(math.log(0.001) - 2.3025852 * jax.random.uniform(splits[4], (FF, RANK), jnp.float32) ** block_scale(splits[4], (FF, RANK), ((0, 16),), -0.2, 0.2)), 0.0001, 0.001)
    return {"inputs": inputs, "grad_out": grad_out, "projection": projection, "moment": moment, "second": second}


def reference(inputs, grad_out, projection, moment, second):
    projected = jnp.dot(inputs, projection, preferred_element_type=jnp.float32).astype(jnp.bfloat16)
    low_rank = lax.dot_general(grad_out, projected, (((0,), (0,)), ((), ())), preferred_element_type=jnp.float32)
    new_moment = 0.9 * moment + 0.1 * low_rank
    new_second = 0.999 * second + 0.001 * (low_rank * low_rank)
    first_fix = 1.0 - 0.9 ** STEP
    second_fix = 1.0 - 0.999 ** STEP
    normalized = (new_moment / first_fix / (jnp.sqrt(new_second / second_fix) + 1e-08)).astype(jnp.bfloat16)
    update = lax.dot_general(projection, normalized, (((1,), (1,)), ((), ())), preferred_element_type=jnp.float32).astype(jnp.bfloat16)
    return (update, new_moment, new_second)
```

```python
import functools

import jax
import jax.numpy as jnp
from jax import lax
from jax.experimental import pallas as pl
from jax.experimental.pallas import tpu as pltpu
from jax.sharding import PartitionSpec as P

STEP = 10
AXES = ("fsdp", "dp")


def bits_of(size):
    return size.bit_length() - 1


def orders(n, m):
    f = [("f", k) for k in range(1, bits_of(n))]
    d = [("d", k) for k in range(bits_of(m))]
    rest = f[1:] + d[1:]
    return (f[:1] + d[:1] + rest, d[:1] + f[:1] + rest)


def gather_orders(n):
    f = [("f", k) for k in range(1, bits_of(n))]
    return (f[::-1], f[:1] + f[:0:-1])


def pairs(n, m, both):
    out = []
    for i in range(n):
        for y in range(m):
            kind, k = both[i & 1]
            j, w = (i ^ (1 << k), y) if kind == "f" else (i, y ^ (1 << k))
            out.append((i * m + y, j * m + w))
    return out


def slot_of(order, block, part, top_first):
    t = 0
    for s, (kind, k) in enumerate(order):
        bit = (block >> (k - 1)) & 1 if kind == "f" else (part >> k) & 1
        t = t + (bit << (len(order) - 1 - s if top_first else s))
    return t


def pick(core, even, odd):
    return jnp.where(core == 0, even, odd)


def project_kernel(n, m, pos, a_ref, b_ref, p_ref, q_ref, g_ref, h_ref, keep_ref, send_ref, left_ref):
    core, own, mine = pos[0], pos[1], pos[2]
    step = pl.program_id(0)
    rows = a_ref.shape[0]
    rank = p_ref.shape[2]
    depth = p_ref.shape[1]

    @pl.when(step == 0)
    def _():
        forder = gather_orders(n)
        for row, x_ref in enumerate((a_ref, b_ref)):
            total = jnp.zeros((rows, rank), jnp.float32)
            for block in range(n // 2):
                for other, w_ref in enumerate((p_ref, q_ref)):
                    owner = core ^ other
                    slot = pick(owner, slot_of(forder[0], block, 0, False), slot_of(forder[1], block, 0, False))
                    start = pl.multiple_of((2 * (own ^ block) + owner) * depth, depth)
                    total += jnp.dot(x_ref[:, pl.ds(start, depth)], w_ref[slot], preferred_element_type=jnp.float32)
            left_ref[:, pl.ds(row * rows, rows)] = total.T.astype(jnp.bfloat16)

    acc = jnp.dot(left_ref[:, :rows], g_ref[...], preferred_element_type=jnp.float32)
    acc += jnp.dot(left_ref[:, rows:], h_ref[...], preferred_element_type=jnp.float32)
    width = keep_ref.shape[2]
    if acc.shape[1] != width:
        acc = pick(core, acc[:, :width], acc[:, width:])
    order = orders(n, m)
    half = keep_ref.shape[0]
    size = rank // m
    for part in range(m):
        rel = part ^ mine
        slot = pick(core, slot_of(order[0], step, rel, True), slot_of(order[1], step, rel, True))
        piece = acc[part * size : (part + 1) * size]

        @pl.when(slot < half)
        def _():
            keep_ref[jnp.minimum(slot, half - 1)] = piece

        @pl.when(slot >= half)
        def _():
            send_ref[jnp.maximum(slot - half, 0)] = piece.astype(jnp.bfloat16)


def expand_kernel(n, m, pos, p_ref, a_ref, b_ref, c_ref, d_ref, o_ref, right_ref):
    core, own, mine = pos[0], pos[1], pos[2]
    block = pl.program_id(0) ^ own
    order = orders(n, m)
    half, size, width = a_ref.shape
    outs = []
    for owner in range(2):
        for part in range(m):
            slot = slot_of(order[owner], block, part ^ mine, True)
            low = jnp.minimum(slot, half - 1)
            high = jnp.maximum(slot - half, 0)
            for same, first, second in ((True, a_ref, b_ref), (False, c_ref, d_ref)):

                @pl.when(jnp.logical_and((core == owner) == same, slot < half))
                def _():
                    right_ref[owner, part * size : (part + 1) * size] = first[low]

                @pl.when(jnp.logical_and((core == owner) == same, slot >= half))
                def _():
                    right_ref[owner, part * size : (part + 1) * size] = second[high]

        outs.append(jnp.dot(p_ref[...], right_ref[owner], preferred_element_type=jnp.float32).astype(o_ref.dtype))
    if width % 128 == 0:
        for owner in range(2):
            o_ref[:, owner * width : (owner + 1) * width] = outs[owner]
    else:
        o_ref[...] = jnp.concatenate(outs, axis=1)


def whole(shape):
    return pl.BlockSpec(shape, lambda s, pos: (0,) * len(shape))


def local(n, m, inputs, grad_out, projection, moment, second):
    i, y = lax.axis_index("fsdp"), lax.axis_index("dp")
    core, own = i & 1, i >> 1
    pos = jnp.stack([core, own, y]).astype(jnp.int32)
    rows = inputs.shape[0]
    width, rank = moment.shape
    size = rank // m
    partner = [(k, k ^ 1) for k in range(n)]

    inputs_too = lax.ppermute(inputs, "fsdp", partner)
    grad_too = lax.ppermute(grad_out, "fsdp", partner)

    held = projection[None]
    forder = gather_orders(n)
    for both in zip(*forder):
        held = jnp.concatenate([held, lax.ppermute(held, AXES, pairs(n, m, both))], axis=0)
    held_too = lax.ppermute(held, "fsdp", partner)

    slots = n // 2 * m
    half = slots // 2
    if width % 128 == 0:
        columns = pl.BlockSpec((rows, width), lambda s, pos: (0, 2 * (s ^ pos[1]) + pos[0]))
    else:
        columns = pl.BlockSpec((rows, 2 * width), lambda s, pos: (0, s ^ pos[1]))
    keep, send = pl.pallas_call(
        functools.partial(project_kernel, n, m),
        grid_spec=pltpu.PrefetchScalarGridSpec(
            num_scalar_prefetch=1,
            grid=(n // 2,),
            in_specs=[
                whole(inputs.shape),
                whole(inputs.shape),
                whole(held.shape),
                whole(held.shape),
                columns,
                columns,
            ],
            out_specs=[whole((half, size, width)), whole((half, size, width))],
            scratch_shapes=[pltpu.VMEM((rank, 2 * rows), jnp.bfloat16)],
        ),
        out_shape=[
            jax.ShapeDtypeStruct((half, size, width), jnp.float32),
            jax.ShapeDtypeStruct((half, size, width), jnp.bfloat16),
        ],
        name="project",
    )(pos, inputs, inputs_too, held, held_too, grad_out, grad_too)

    steps = list(zip(*orders(n, m)))
    for s, both in enumerate(steps):
        got = lax.ppermute(send, AXES, pairs(n, m, both)).astype(jnp.float32)
        if s + 1 < len(steps):
            cut = keep.shape[0] // 2
            send = (keep[cut:] + got[cut:]).astype(jnp.bfloat16)
            keep = keep[:cut] + got[:cut]
        else:
            low_rank = (keep + got)[0]

    moment_t, second_t = moment.T, second.T
    first_fix = 1.0 - 0.9**STEP
    second_fix = 1.0 - 0.999**STEP
    new_m = 0.9 * lax.dynamic_slice_in_dim(moment_t, y * size, size) + 0.1 * low_rank
    new_s = 0.999 * lax.dynamic_slice_in_dim(second_t, y * size, size) + 0.001 * (low_rank * low_rank)
    normalized = (new_m / first_fix / (jnp.sqrt(new_s / second_fix) + 1e-08)).astype(jnp.bfloat16)

    held = normalized[None]
    for both in steps[:0:-1]:
        held = jnp.concatenate([held, lax.ppermute(held, AXES, pairs(n, m, both))], axis=0)
    rest = lax.ppermute(held, AXES, pairs(n, m, steps[0]))
    held_too = lax.ppermute(held, "fsdp", partner)
    rest_too = lax.ppermute(rest, "fsdp", partner)

    update = pl.pallas_call(
        functools.partial(expand_kernel, n, m),
        grid_spec=pltpu.PrefetchScalarGridSpec(
            num_scalar_prefetch=1,
            grid=(n // 2,),
            in_specs=[whole(projection.shape)] + [whole(held.shape)] * 4,
            out_specs=pl.BlockSpec((projection.shape[0], 2 * width), lambda s, pos: (0, s)),
            scratch_shapes=[pltpu.VMEM((2, rank, width), jnp.bfloat16)],
        ),
        out_shape=jax.ShapeDtypeStruct((projection.shape[0], n * width), jnp.bfloat16),
        name="expand",
    )(pos, projection, held, rest, held_too, rest_too)

    full = low_rank
    for k in range(bits_of(m)):
        got = lax.ppermute(full, "dp", [(w, w ^ (1 << k)) for w in range(m)])
        first = ((y >> k) & 1) == 0
        full = jnp.concatenate([jnp.where(first, full, got), jnp.where(first, got, full)], axis=0)
    full = full.T
    new_moment = 0.9 * moment + 0.1 * full
    new_second = 0.999 * second + 0.001 * (full * full)
    return (update, new_moment, new_second)


def solution(mesh):
    in_specs = (
        P(AXES, None),
        P(AXES, None),
        P("fsdp", None),
        P("fsdp", None),
        P("fsdp", None),
    )
    out_specs = (P("fsdp", None), P("fsdp", None), P("fsdp", None))
    body = functools.partial(local, mesh.shape["fsdp"], mesh.shape["dp"])
    return jax.shard_map(body, mesh=mesh, in_specs=in_specs, out_specs=out_specs, check_vma=False)
```

```python
import functools

import jax
import jax.numpy as jnp
from jax import lax
from jax.experimental import pallas as pl
from jax.experimental.pallas import tpu as pltpu
from jax.sharding import PartitionSpec as P

STEP = 10
AXES = ("fsdp", "dp")


def bits_of(size):
    return size.bit_length() - 1


def orders(n, m):
    f = [("f", k) for k in range(1, bits_of(n))]
    d = [("d", k) for k in range(bits_of(m))]
    even = f[:1] + d[:1] + f[1:] + d[1:]
    odd = d[:1] + f[1:2] + f[:1] + f[2:] + d[1:]
    return even, odd


def gather_plan(n):
    plan = []
    for block in sorted(range(1, n // 2), key=lambda b: (b.bit_count(), -b)):
        low = block & -block
        via = low if block.bit_count() < 3 else (block ^ low) & -(block ^ low)
        plan.append((block, block ^ via, bits_of(via) + 1))
    return plan


def chunks_of(width):
    tiles = width // 128
    if width % 128 or tiles < 2:
        return ((0, width),)
    cut = tiles // 2 * 128
    return ((0, cut), (cut, width))


def pairs(n, m, both):
    out = []
    for i in range(n):
        for y in range(m):
            kind, k = both[i & 1]
            j, w = (i ^ (1 << k), y) if kind == "f" else (i, y ^ (1 << k))
            out.append((i * m + y, j * m + w))
    return out


def slot_of(order, block, part):
    t = 0
    for kind, k in order:
        t = 2 * t + ((block >> (k - 1)) & 1 if kind == "f" else (part >> k) & 1)
    return t


def state_kernel(moment_ref, second_ref, *refs):
    fulls, (new_m_ref, new_s_ref) = refs[:-2], refs[-2:]
    full = jnp.concatenate([full[...] for full in fulls], axis=1).T
    new_m_ref[...] = 0.9 * moment_ref[...] + 0.1 * full
    new_s_ref[...] = 0.999 * second_ref[...] + 0.001 * (full * full)


def project_kernel(n, m, width, a_hbm, own_hbm, g_hbm, b_ref, *refs):
    blocks, h_ref, outs, (a_ref, own_ref, g_ref, sems) = refs[: n - 1], refs[n - 1], refs[n:-4], refs[-4:]
    i, mine = lax.axis_index("fsdp"), lax.axis_index("dp")
    core, own = i & 1, i >> 1
    depth, rank = own_ref.shape
    half, size, _ = outs[0].shape
    rows = b_ref.shape[0]
    span = g_ref.shape[2]

    def columns_of(block):
        start = (2 * (block ^ own) + core) * width if span == width else (block ^ own) * span
        return pl.ds(pl.multiple_of(start, 128), span)

    first = [
        pltpu.make_async_copy(own_hbm, own_ref, sems.at[n // 2]),
        pltpu.make_async_copy(a_hbm, a_ref, sems.at[n // 2 + 1]),
    ]
    loads = [
        pltpu.make_async_copy(g_hbm.at[:, columns_of(block)], g_ref.at[block], sems.at[block])
        for block in range(n // 2)
    ]
    for load in first + loads:
        load.start()

    left = []
    for x_ref, load in zip((b_ref, a_ref), first):
        total = jnp.zeros((rows, rank), jnp.float32)
        if x_ref is a_ref:
            load.wait()
        for k in (*range(1, n), 0):
            if k == 0 and x_ref is b_ref:
                load.wait()
            w_ref = blocks[k - 1] if k else own_ref
            start = pl.multiple_of((2 * (own ^ (k >> 1)) + (core ^ (k & 1))) * depth, depth)
            total += jnp.dot(x_ref[:, pl.ds(start, depth)], w_ref[...], preferred_element_type=jnp.float32)
        total = total.T
        for k in range(bits_of(m)):
            swapped = [total[(p ^ (1 << k)) * size :][:size] for p in range(m)]
            total = jnp.where(((mine >> k) & 1) == 0, total, jnp.concatenate(swapped, axis=0))
        left.append(total.astype(jnp.bfloat16))

    def columns(c):
        for block in range(n // 2):
            acc = jnp.dot(left[0], h_ref[:, columns_of(block)], preferred_element_type=jnp.float32)
            loads[block].wait()
            acc += jnp.dot(left[1], g_ref[block], preferred_element_type=jnp.float32)
            if span != width:
                acc = acc[:, c * width : (c + 1) * width]
            for part in range(m):
                slot = slot_of(orders(n, m)[c], block, part)
                for (first, last), keep_ref, send_ref in zip(chunks_of(width), outs[::2], outs[1::2]):
                    piece = acc[part * size : (part + 1) * size, first:last]
                    if slot < half:
                        keep_ref[slot] = piece
                    else:
                        send_ref[slot - half] = piece.astype(jnp.bfloat16)

    for c in range(2):
        pl.when(core == c)(functools.partial(columns, c))


def expand_kernel(n, m, width, p_ref, *refs):
    parts, (o_ref, stage_ref, sems) = refs[:-3], refs[-3:]
    i = lax.axis_index("fsdp")
    core, own = i & 1, i >> 1
    half = parts[0].shape[0]
    paired = width % 128 != 0

    def rows(c):
        copies = []
        for block in range(n // 2):
            pair = []
            for owner in range(2):
                outs = []
                for k in range(len(chunks_of(width))):
                    mine = parts[4 * k : 4 * k + 2] if owner == c else parts[4 * k + 2 : 4 * k + 4]
                    slots = [slot_of(orders(n, m)[owner], block, part) for part in range(m)]
                    right = jnp.concatenate([mine[t // half][t % half] for t in slots], axis=0)
                    out = jnp.dot(p_ref[...], right, preferred_element_type=jnp.float32)
                    outs.append(out.astype(o_ref.dtype))
                pair.append(outs[0] if len(outs) == 1 else jnp.concatenate(outs, axis=1))
            whole = [jnp.concatenate(pair, axis=1)] if paired else pair
            for owner, out in enumerate(whole):
                k = block * len(whole) + owner
                start = (block ^ own) * 2 * width + owner * width
                stage_ref[k] = out
                copy = pltpu.make_async_copy(
                    stage_ref.at[k], o_ref.at[:, pl.ds(pl.multiple_of(start, 128), out.shape[1])], sems.at[k]
                )
                copy.start()
                copies.append(copy)
        for copy in copies:
            copy.wait()

    for c in range(2):
        pl.when(core == c)(functools.partial(rows, c))


def relative_ranks(x, y, m):
    size = x.shape[1] // m
    for k in range(bits_of(m)):
        swapped = jnp.concatenate([x[:, (p ^ (1 << k)) * size :][:, :size] for p in range(m)], axis=1)
        x = jnp.where(((y >> k) & 1) == 0, x, swapped)
    return x


def placed(space, *arrays):
    return [pltpu.with_memory_space_constraint(x, space) for x in arrays]


VMEM = pl.BlockSpec(memory_space=pltpu.VMEM)
HBM = pl.BlockSpec(memory_space=pltpu.HBM)


def local(n, m, inputs, grad_out, projection, moment, second):
    y = lax.axis_index("dp")
    width, rank = moment.shape
    size = rank // m
    partner = [(k, k ^ 1) for k in range(n)]

    inputs_too = lax.ppermute(inputs, "fsdp", partner)
    grad_too = lax.ppermute(grad_out, "fsdp", partner)

    held = {0: projection}
    held_too = {0: lax.ppermute(projection, "fsdp", partner)}
    for block, source, k in gather_plan(n):
        held[block] = lax.ppermute(held[source], "fsdp", [(w, w ^ (1 << k)) for w in range(n)])
        held_too[block] = lax.ppermute(held[block], "fsdp", partner)
    blocks = [x for block in range(n // 2) for x in (held[block], held_too[block])]

    half = n // 2 * m // 2
    shapes = [
        pltpu.VMEM((half, size, stop - start), dtype)
        for start, stop in chunks_of(width)
        for dtype in (jnp.float32, jnp.bfloat16)
    ]
    sums = pl.pallas_call(
        functools.partial(project_kernel, n, m, width),
        in_specs=[HBM] * 3 + [VMEM] * (n + 1),
        out_specs=[VMEM] * len(shapes),
        out_shape=shapes,
        scratch_shapes=[
            pltpu.VMEM(inputs.shape, inputs.dtype),
            pltpu.VMEM(projection.shape, projection.dtype),
            pltpu.VMEM((n // 2, inputs.shape[0], width if width % 128 == 0 else 2 * width), grad_out.dtype),
            pltpu.SemaphoreType.DMA((n // 2 + 2,)),
        ],
        compiler_params=pltpu.CompilerParams(vmem_limit_bytes=16 << 20),
        name="project",
    )(
        *placed(pltpu.HBM, inputs, projection, grad_out),
        *placed(pltpu.VMEM, inputs_too, *blocks[1:], grad_too),
    )

    moment_t = lax.dynamic_slice_in_dim(moment.T, y * size, size)
    second_t = lax.dynamic_slice_in_dim(second.T, y * size, size)
    first_fix = 1.0 - 0.9**STEP
    second_fix = 1.0 - 0.999**STEP
    steps = list(zip(*orders(n, m)))
    parts, fulls = [], []
    for chunk, (start, stop) in enumerate(chunks_of(width)):
        keep, send = sums[2 * chunk : 2 * chunk + 2]
        for s, both in enumerate(steps):
            got = lax.ppermute(send, AXES, pairs(n, m, both)).astype(jnp.float32)
            if s + 1 < len(steps):
                cut = keep.shape[0] // 2
                send = (keep[cut:] + got[cut:]).astype(jnp.bfloat16)
                keep = keep[:cut] + got[:cut]
            else:
                low_rank = (keep + got)[0]

        new_m = 0.9 * moment_t[:, start:stop] + 0.1 * low_rank
        new_s = 0.999 * second_t[:, start:stop] + 0.001 * (low_rank * low_rank)
        normalized = (new_m / first_fix / (jnp.sqrt(new_s / second_fix) + 1e-08)).astype(jnp.bfloat16)

        full = low_rank
        for k in range(bits_of(m)):
            got = lax.ppermute(full, "dp", [(w, w ^ (1 << k)) for w in range(m)])
            first = ((y >> k) & 1) == 0
            full = jnp.concatenate([jnp.where(first, full, got), jnp.where(first, got, full)], axis=0)

        held = normalized[None]
        for both in steps[:0:-1]:
            got = lax.ppermute(held, AXES, pairs(n, m, both))
            held = jnp.concatenate([held, got], axis=0)
        fulls.append(full)
        if stop == width:
            new_moment, new_second = pl.pallas_call(
                state_kernel,
                out_shape=[jax.ShapeDtypeStruct(moment.shape, jnp.float32)] * 2,
                compiler_params=pltpu.CompilerParams(vmem_limit_bytes=16 << 20),
                name="state",
            )(moment, second, *fulls)
        rest = lax.ppermute(held, AXES, pairs(n, m, steps[0]))
        if stop == width:
            rest, new_moment, new_second = lax.optimization_barrier((rest, new_moment, new_second))
        parts += [held, rest, lax.ppermute(held, "fsdp", partner), lax.ppermute(rest, "fsdp", partner)]

    copies = n if width % 128 == 0 else n // 2
    update = pl.pallas_call(
        functools.partial(expand_kernel, n, m, width),
        in_specs=[VMEM] * (1 + len(parts)),
        out_specs=HBM,
        out_shape=jax.ShapeDtypeStruct((projection.shape[0], n * width), jnp.bfloat16),
        scratch_shapes=[
            pltpu.VMEM((copies, projection.shape[0], n * width // copies), jnp.bfloat16),
            pltpu.SemaphoreType.DMA((copies,)),
        ],
        compiler_params=pltpu.CompilerParams(vmem_limit_bytes=16 << 20),
        name="expand",
    )(*placed(pltpu.VMEM, relative_ranks(projection, y, m), *parts))
    return (update, new_moment, new_second)


def solution(mesh):
    in_specs = (
        P(AXES, None),
        P(AXES, None),
        P("fsdp", None),
        P("fsdp", None),
        P("fsdp", None),
    )
    out_specs = (P("fsdp", None), P("fsdp", None), P("fsdp", None))

    def body(*args):
        return local(mesh.shape["fsdp"], mesh.shape["dp"], *args)

    return jax.shard_map(body, mesh=mesh, in_specs=in_specs, out_specs=out_specs, check_vma=False)
```

```python
import functools

import jax
import jax.numpy as jnp
from jax import lax
from jax.experimental import pallas as pl
from jax.experimental.pallas import tpu as pltpu
from jax.sharding import PartitionSpec as P

STEP = 10
ORDERS = (("zyxw", "zxyw"), ("xzyw", "yxzw"))
EXPAND = (1, 0)
AXES = ("fsdp", "dp")


def bits_of(size):
    return size.bit_length() - 1


def orders(n, m, chunk):
    f = [("f", k) for k in range(1, bits_of(n))]
    d = [("d", k) for k in range(bits_of(m))]
    bits = dict(x=f[:1], y=d[:1], z=f[1:2], w=f[2:])
    return tuple([bit for axis in order for bit in bits[axis]] + d[1:] for order in ORDERS[chunk])


def gather_plan(n):
    plan = []
    for block in sorted(range(1, n // 2), key=lambda b: (b.bit_count(), -b)):
        low = block & -block
        via = low if block.bit_count() < 3 else (block ^ low) & -(block ^ low)
        plan.append((block, block ^ via, bits_of(via) + 1))
    return plan


def chunks_of(width):
    tiles = width // 128
    if width % 128 or tiles < 2:
        return ((0, width),)
    cut = (tiles - 1) // 2 * 128
    return ((0, cut), (cut, width))


def pairs(n, m, both):
    out = []
    for i in range(n):
        for y in range(m):
            kind, k = both[i & 1]
            j, w = (i ^ (1 << k), y) if kind == "f" else (i, y ^ (1 << k))
            out.append((i * m + y, j * m + w))
    return out


def slot_of(order, block, part):
    t = 0
    for kind, k in order:
        t = 2 * t + ((block >> (k - 1)) & 1 if kind == "f" else (part >> k) & 1)
    return t


def state_kernel(moment_ref, second_ref, *refs):
    fulls, (new_m_ref, new_s_ref) = refs[:-2], refs[-2:]
    full = jnp.concatenate([full[...] for full in fulls], axis=1).T
    new_m_ref[...] = 0.9 * moment_ref[...] + 0.1 * full
    new_s_ref[...] = 0.999 * second_ref[...] + 0.001 * (full * full)


def start_columns(n, width, chunk, g_hbm, g_ref, sems):
    i = lax.axis_index("fsdp")
    loads = []
    for block in range(n // 2):
        at = columns_of(width, chunk, block ^ (i >> 1), i & 1)
        loads.append(pltpu.make_async_copy(g_hbm.at[:, at], g_ref.at[block], sems.at[block]))
        loads[-1].start()
    return loads


def columns_of(width, chunk, block, core):
    if width % 128:
        return pl.ds(pl.multiple_of(block * 2 * width, 128), 2 * width)
    first, last = chunks_of(width)[chunk]
    return pl.ds(pl.multiple_of((2 * block + core) * width + first, 128), last - first)


def multiply(n, m, width, chunk, left_ref, loads, g_ref, h_ref, keep_ref, send_ref):
    i = lax.axis_index("fsdp")
    core, own = i & 1, i >> 1
    half, size, _ = keep_ref.shape

    def columns(c):
        for block in range(n // 2):
            at = columns_of(width, chunk, block ^ own, c)
            acc = jnp.dot(left_ref[1], h_ref[:, at], preferred_element_type=jnp.float32)
            loads[block].wait()
            acc += jnp.dot(left_ref[0], g_ref[block], preferred_element_type=jnp.float32)
            if width % 128:
                acc = acc[:, c * width : (c + 1) * width]
            for part in range(m):
                slot = slot_of(orders(n, m, chunk)[c], block, part)
                piece = acc[part * size : (part + 1) * size]
                if slot < half:
                    keep_ref[slot] = piece
                else:
                    send_ref[slot - half] = piece.astype(jnp.bfloat16)

    for c in range(2):
        pl.when(core == c)(functools.partial(columns, c))


def first_kernel(n, m, width, a_hbm, own_hbm, g_hbm, b_ref, *refs):
    blocks, h_ref, (keep_ref, send_ref, left_ref, a_ref, own_ref, g_ref, sems) = refs[: n - 1], refs[n - 1], refs[n:]
    i, mine = lax.axis_index("fsdp"), lax.axis_index("dp")
    core, own = i & 1, i >> 1
    depth, rank = own_ref.shape
    rows = b_ref.shape[0]
    size = rank // m
    copies = [
        pltpu.make_async_copy(own_hbm, own_ref, sems.at[n // 2]),
        pltpu.make_async_copy(a_hbm, a_ref, sems.at[n // 2 + 1]),
    ]
    for copy in copies:
        copy.start()
    loads = start_columns(n, width, 0, g_hbm, g_ref, sems)
    for place, x_ref in ((1, b_ref), (0, a_ref)):
        total = jnp.zeros((rows, rank), jnp.float32)
        if x_ref is a_ref:
            copies[1].wait()
        for k in (*range(1, n), 0):
            if k == 0 and x_ref is b_ref:
                copies[0].wait()
            w_ref = blocks[k - 1] if k else own_ref
            start = pl.multiple_of((2 * (own ^ (k >> 1)) + (core ^ (k & 1))) * depth, depth)
            total += jnp.dot(x_ref[:, pl.ds(start, depth)], w_ref[...], preferred_element_type=jnp.float32)
        total = total.T
        for k in range(bits_of(m)):
            swapped = [total[(p ^ (1 << k)) * size :][:size] for p in range(m)]
            total = jnp.where(((mine >> k) & 1) == 0, total, jnp.concatenate(swapped, axis=0))
        left_ref[place] = total.astype(jnp.bfloat16)
    multiply(n, m, width, 0, left_ref, loads, g_ref, h_ref, keep_ref, send_ref)


def next_kernel(n, m, width, chunk, g_hbm, h_ref, left_ref, keep_ref, send_ref, g_ref, sems):
    loads = start_columns(n, width, chunk, g_hbm, g_ref, sems)
    multiply(n, m, width, chunk, left_ref, loads, g_ref, h_ref, keep_ref, send_ref)


def expand_kernel(n, m, width, chunk, p_ref, *refs):
    parts, (o_ref, stage_ref, sems) = refs[:4], refs[-3:]
    i = lax.axis_index("fsdp")
    core, own = i & 1, i >> 1
    half = parts[0].shape[0]

    def rows(c):
        copies = []
        for block in range(n // 2):
            pair = []
            for owner in range(2):
                mine = parts[:2] if owner == c else parts[2:]
                slots = [slot_of(orders(n, m, chunk)[owner], block, part) for part in range(m)]
                right = jnp.concatenate([mine[t // half][t % half] for t in slots], axis=0)
                out = jnp.dot(p_ref[...], right, preferred_element_type=jnp.float32)
                pair.append(out.astype(o_ref.dtype))
            whole = [jnp.concatenate(pair, axis=1)] if width % 128 else pair
            for owner, out in enumerate(whole):
                k = block * len(whole) + owner
                stage_ref[k] = out
                at = columns_of(width, chunk, block ^ own, owner)
                copies.append(pltpu.make_async_copy(stage_ref.at[k], o_ref.at[:, at], sems.at[k]))
                copies[-1].start()
        for copy in copies:
            copy.wait()

    for c in range(2):
        pl.when(core == c)(functools.partial(rows, c))


def relative_ranks(x, y, m):
    size = x.shape[1] // m
    for k in range(bits_of(m)):
        swapped = jnp.concatenate([x[:, (p ^ (1 << k)) * size :][:, :size] for p in range(m)], axis=1)
        x = jnp.where(((y >> k) & 1) == 0, x, swapped)
    return x


def placed(space, *arrays):
    return [pltpu.with_memory_space_constraint(x, space) for x in arrays]


VMEM = pl.BlockSpec(memory_space=pltpu.VMEM)
HBM = pl.BlockSpec(memory_space=pltpu.HBM)


def local(n, m, inputs, grad_out, projection, moment, second):
    y = lax.axis_index("dp")
    width, rank = moment.shape
    rows = inputs.shape[0]
    size = rank // m
    partner = [(k, k ^ 1) for k in range(n)]

    inputs_too = lax.ppermute(inputs, "fsdp", partner)
    grad_too = lax.ppermute(grad_out, "fsdp", partner)

    held = {0: projection}
    held_too = {0: lax.ppermute(projection, "fsdp", partner)}
    for block, source, k in gather_plan(n):
        held[block] = lax.ppermute(held[source], "fsdp", [(w, w ^ (1 << k)) for w in range(n)])
        held_too[block] = lax.ppermute(held[block], "fsdp", partner)
    blocks = [x for block in range(n // 2) for x in (held[block], held_too[block])]

    half = n // 2 * m // 2
    sums, left = [], None
    for chunk, (start, stop) in enumerate(chunks_of(width)):
        span = stop - start if width % 128 == 0 else 2 * width
        shapes = [
            pltpu.VMEM((half, size, stop - start), jnp.float32),
            pltpu.VMEM((half, size, stop - start), jnp.bfloat16),
        ]
        held_columns = pltpu.VMEM((n // 2, rows, span), grad_out.dtype)
        params = pltpu.CompilerParams(vmem_limit_bytes=16 << 20)
        if left is None:
            *pair, left = pl.pallas_call(
                functools.partial(first_kernel, n, m, width),
                in_specs=[HBM] * 3 + [VMEM] * (n + 1),
                out_specs=[VMEM] * 3,
                out_shape=shapes + [pltpu.VMEM((2, rank, rows), jnp.bfloat16)],
                scratch_shapes=[
                    pltpu.VMEM(inputs.shape, inputs.dtype),
                    pltpu.VMEM(projection.shape, projection.dtype),
                    held_columns,
                    pltpu.SemaphoreType.DMA((n // 2 + 2,)),
                ],
                compiler_params=params,
                name="project",
            )(
                *placed(pltpu.HBM, inputs, projection, grad_out),
                *placed(pltpu.VMEM, inputs_too, *blocks[1:], grad_too),
            )
        else:
            pair = pl.pallas_call(
                functools.partial(next_kernel, n, m, width, chunk),
                in_specs=[HBM] + [VMEM] * 2,
                out_specs=[VMEM] * 2,
                out_shape=shapes,
                scratch_shapes=[held_columns, pltpu.SemaphoreType.DMA((n // 2,))],
                compiler_params=params,
                name="multiply",
            )(*placed(pltpu.HBM, grad_out), *placed(pltpu.VMEM, grad_too, left))
        sums += pair

    moment_t = lax.dynamic_slice_in_dim(moment.T, y * size, size)
    second_t = lax.dynamic_slice_in_dim(second.T, y * size, size)
    first_fix = 1.0 - 0.9**STEP
    second_fix = 1.0 - 0.999**STEP
    parts, fulls = [], []
    for chunk, (start, stop) in enumerate(chunks_of(width)):
        steps = list(zip(*orders(n, m, chunk)))
        keep, send = sums[2 * chunk : 2 * chunk + 2]
        for s, both in enumerate(steps):
            got = lax.ppermute(send, AXES, pairs(n, m, both)).astype(jnp.float32)
            if s + 1 < len(steps):
                cut = keep.shape[0] // 2
                send = (keep[cut:] + got[cut:]).astype(jnp.bfloat16)
                keep = keep[:cut] + got[:cut]
            else:
                low_rank = (keep + got)[0]

        new_m = 0.9 * moment_t[:, start:stop] + 0.1 * low_rank
        new_s = 0.999 * second_t[:, start:stop] + 0.001 * (low_rank * low_rank)
        normalized = (new_m / first_fix / (jnp.sqrt(new_s / second_fix) + 1e-08)).astype(jnp.bfloat16)

        full = low_rank
        for k in range(bits_of(m)):
            got = lax.ppermute(full, "dp", [(w, w ^ (1 << k)) for w in range(m)])
            first = ((y >> k) & 1) == 0
            full = jnp.concatenate([jnp.where(first, full, got), jnp.where(first, got, full)], axis=0)

        held = normalized[None]
        for both in steps[:0:-1]:
            got = lax.ppermute(held, AXES, pairs(n, m, both))
            held = jnp.concatenate([held, got], axis=0)
        fulls.append(full)
        if stop == width:
            new_moment, new_second = pl.pallas_call(
                state_kernel,
                out_shape=[jax.ShapeDtypeStruct(moment.shape, jnp.float32)] * 2,
                compiler_params=pltpu.CompilerParams(vmem_limit_bytes=16 << 20),
                name="state",
            )(moment, second, *fulls)
        rest = lax.ppermute(held, AXES, pairs(n, m, steps[0]))
        if stop == width:
            rest, new_moment, new_second = lax.optimization_barrier((rest, new_moment, new_second))
        parts.append([held, rest, lax.ppermute(held, "fsdp", partner), lax.ppermute(rest, "fsdp", partner)])

    copies = n if width % 128 == 0 else n // 2
    relative = relative_ranks(projection, y, m)
    update = []
    for chunk in EXPAND[-len(parts) :]:
        start, stop = chunks_of(width)[chunk]
        update = [
            pl.pallas_call(
                functools.partial(expand_kernel, n, m, width, chunk),
                in_specs=[VMEM] * 5 + [HBM] * len(update),
                out_specs=HBM,
                out_shape=jax.ShapeDtypeStruct((projection.shape[0], n * width), jnp.bfloat16),
                input_output_aliases={5: 0} if update else {},
                scratch_shapes=[
                    pltpu.VMEM((copies, projection.shape[0], n * (stop - start) // copies), jnp.bfloat16),
                    pltpu.SemaphoreType.DMA((copies,)),
                ],
                compiler_params=pltpu.CompilerParams(vmem_limit_bytes=16 << 20),
                name="expand",
            )(*placed(pltpu.VMEM, relative, *parts[chunk]), *update)
        ]
    return (*update, new_moment, new_second)


def solution(mesh):
    in_specs = (
        P(AXES, None),
        P(AXES, None),
        P("fsdp", None),
        P("fsdp", None),
        P("fsdp", None),
    )
    out_specs = (P("fsdp", None), P("fsdp", None), P("fsdp", None))

    def body(*args):
        return local(mesh.shape["fsdp"], mesh.shape["dp"], *args)

    return jax.shard_map(body, mesh=mesh, in_specs=in_specs, out_specs=out_specs, check_vma=False)
```

```python
import functools

import jax
import jax.numpy as jnp
from jax import lax
from jax.experimental import pallas as pl
from jax.experimental.pallas import tpu as pltpu
from jax.sharding import PartitionSpec as P

STEP = 10
ORDERS = (("zxyw", "zxyw"), ("xzyw", "yxzw"))
AXES = ("fsdp", "dp")


def bits_of(size):
    return size.bit_length() - 1


def orders(n, m, chunk):
    f = [("f", k) for k in range(1, bits_of(n))]
    d = [("d", k) for k in range(bits_of(m))]
    bits = dict(x=f[:1], y=d[:1], z=f[1:2], w=f[2:])
    return tuple([bit for axis in order for bit in bits[axis]] + d[1:] for order in ORDERS[chunk])


def gather_plan(n):
    plan = []
    for block in sorted(range(1, n // 2), key=lambda b: (b.bit_count(), -b)):
        low = block & -block
        via = low if block.bit_count() < 3 else (block ^ low) & -(block ^ low)
        plan.append((block, block ^ via, bits_of(via) + 1))
    return plan


def chunks_of(width):
    tiles = width // 128
    if width % 128 or tiles < 2:
        return ((0, width),)
    cut = (tiles - 1) // 2 * 128
    return ((0, cut), (cut, width))


def pairs(n, m, both):
    out = []
    for i in range(n):
        for y in range(m):
            kind, k = both[i & 1]
            j, w = (i ^ (1 << k), y) if kind == "f" else (i, y ^ (1 << k))
            out.append((i * m + y, j * m + w))
    return out


def slot_of(order, block, part):
    t = 0
    for kind, k in order:
        t = 2 * t + ((block >> (k - 1)) & 1 if kind == "f" else (part >> k) & 1)
    return t


def state_kernel(moment_ref, second_ref, *refs):
    fulls, (new_m_ref, new_s_ref) = refs[:-2], refs[-2:]
    full = jnp.concatenate([full[...] for full in fulls], axis=1).T
    new_m_ref[...] = 0.9 * moment_ref[...] + 0.1 * full
    new_s_ref[...] = 0.999 * second_ref[...] + 0.001 * (full * full)


def start_columns(n, width, chunk, g_hbm, g_ref, sems):
    i = lax.axis_index("fsdp")
    loads = []
    for block in range(n // 2):
        at = columns_of(width, chunk, block ^ (i >> 1), i & 1)
        loads.append(pltpu.make_async_copy(g_hbm.at[:, at], g_ref.at[block], sems.at[block]))
        loads[-1].start()
    return loads


def columns_of(width, chunk, block, core):
    if width % 128:
        return pl.ds(pl.multiple_of(block * 2 * width, 128), 2 * width)
    first, last = chunks_of(width)[chunk]
    return pl.ds(pl.multiple_of((2 * block + core) * width + first, 128), last - first)


def multiply(n, m, width, chunk, left_ref, loads, g_ref, h_ref, keep_ref, send_ref):
    i = lax.axis_index("fsdp")
    core, own = i & 1, i >> 1
    half, size, _ = keep_ref.shape

    def columns(c):
        for block in range(n // 2):
            at = columns_of(width, chunk, block ^ own, c)
            acc = jnp.dot(left_ref[1], h_ref[:, at], preferred_element_type=jnp.float32)
            loads[block].wait()
            acc += jnp.dot(left_ref[0], g_ref[block], preferred_element_type=jnp.float32)
            if width % 128:
                acc = acc[:, c * width : (c + 1) * width]
            for part in range(m):
                slot = slot_of(orders(n, m, chunk)[c], block, part)
                piece = acc[part * size : (part + 1) * size]
                if slot < half:
                    keep_ref[slot] = piece
                else:
                    send_ref[slot - half] = piece.astype(jnp.bfloat16)

    for c in range(2):
        pl.when(core == c)(functools.partial(columns, c))


def first_kernel(n, m, width, a_hbm, own_hbm, g_hbm, b_ref, *refs):
    blocks, h_ref, (keep_ref, send_ref, left_ref, a_ref, own_ref, g_ref, sems) = refs[: n - 1], refs[n - 1], refs[n:]
    i, mine = lax.axis_index("fsdp"), lax.axis_index("dp")
    core, own = i & 1, i >> 1
    depth, rank = own_ref.shape
    rows = b_ref.shape[0]
    size = rank // m
    copies = [
        pltpu.make_async_copy(own_hbm, own_ref, sems.at[n // 2]),
        pltpu.make_async_copy(a_hbm, a_ref, sems.at[n // 2 + 1]),
    ]
    for copy in copies:
        copy.start()
    loads = start_columns(n, width, 0, g_hbm, g_ref, sems)
    for place, x_ref in ((1, b_ref), (0, a_ref)):
        total = jnp.zeros((rows, rank), jnp.float32)
        if x_ref is a_ref:
            copies[1].wait()
        for k in (*range(1, n), 0):
            if k == 0 and x_ref is b_ref:
                copies[0].wait()
            w_ref = blocks[k - 1] if k else own_ref
            start = pl.multiple_of((2 * (own ^ (k >> 1)) + (core ^ (k & 1))) * depth, depth)
            total += jnp.dot(x_ref[:, pl.ds(start, depth)], w_ref[...], preferred_element_type=jnp.float32)
        total = total.T
        for k in range(bits_of(m)):
            swapped = [total[(p ^ (1 << k)) * size :][:size] for p in range(m)]
            total = jnp.where(((mine >> k) & 1) == 0, total, jnp.concatenate(swapped, axis=0))
        left_ref[place] = total.astype(jnp.bfloat16)
    multiply(n, m, width, 0, left_ref, loads, g_ref, h_ref, keep_ref, send_ref)


def next_kernel(n, m, width, chunk, g_hbm, h_ref, left_ref, keep_ref, send_ref, g_ref, sems):
    loads = start_columns(n, width, chunk, g_hbm, g_ref, sems)
    multiply(n, m, width, chunk, left_ref, loads, g_ref, h_ref, keep_ref, send_ref)


def expand_kernel(n, m, width, whose, p_ref, *refs):
    count = len(chunks_of(width))
    parts, (o_ref, stage_ref, sems) = refs[: 2 * count * len(whose)], refs[-3:]
    i = lax.axis_index("fsdp")
    core, own = i & 1, i >> 1
    half = parts[0].shape[0]

    def rows(c):
        copies = []
        for block in range(n // 2):
            outs = {}
            for k, other in enumerate(whose):
                owner = c ^ other
                columns = []
                for chunk in range(count):
                    first = 2 * (k * count + chunk)
                    order = orders(n, m, chunk)[owner]
                    slots = [slot_of(order, block, part) for part in range(m)]
                    right = jnp.concatenate([parts[first + t // half][t % half] for t in slots], axis=0)
                    out = jnp.dot(p_ref[...], right, preferred_element_type=jnp.float32)
                    columns.append(out.astype(o_ref.dtype))
                outs[owner] = columns
            if width % 128:
                stage_ref[block] = jnp.concatenate(outs[0] + outs[1], axis=1)
                at = pl.ds(pl.multiple_of((block ^ own) * 2 * width, 128), 2 * width)
            else:
                ((owner, columns),) = outs.items()
                for (first, last), out in zip(chunks_of(width), columns):
                    stage_ref[block, :, first:last] = out
                at = pl.ds(pl.multiple_of((2 * (block ^ own) + owner) * width, 128), width)
            copies.append(pltpu.make_async_copy(stage_ref.at[block], o_ref.at[:, at], sems.at[block]))
            copies[-1].start()
        for copy in copies:
            copy.wait()

    for c in range(2):
        pl.when(core == c)(functools.partial(rows, c))


def relative_ranks(x, y, m):
    size = x.shape[1] // m
    for k in range(bits_of(m)):
        swapped = jnp.concatenate([x[:, (p ^ (1 << k)) * size :][:, :size] for p in range(m)], axis=1)
        x = jnp.where(((y >> k) & 1) == 0, x, swapped)
    return x


def placed(space, *arrays):
    return [pltpu.with_memory_space_constraint(x, space) for x in arrays]


VMEM = pl.BlockSpec(memory_space=pltpu.VMEM)
HBM = pl.BlockSpec(memory_space=pltpu.HBM)


def local(n, m, inputs, grad_out, projection, moment, second):
    y = lax.axis_index("dp")
    width, rank = moment.shape
    rows = inputs.shape[0]
    size = rank // m
    partner = [(k, k ^ 1) for k in range(n)]

    inputs_too = lax.ppermute(inputs, "fsdp", partner)
    grad_too = lax.ppermute(grad_out, "fsdp", partner)

    held = {0: projection}
    held_too = {0: lax.ppermute(projection, "fsdp", partner)}
    for block, source, k in gather_plan(n):
        held[block] = lax.ppermute(held[source], "fsdp", [(w, w ^ (1 << k)) for w in range(n)])
        held_too[block] = lax.ppermute(held[block], "fsdp", partner)
    blocks = [x for block in range(n // 2) for x in (held[block], held_too[block])]

    half = n // 2 * m // 2
    sums, left = [], None
    for chunk, (start, stop) in enumerate(chunks_of(width)):
        span = stop - start if width % 128 == 0 else 2 * width
        shapes = [
            pltpu.VMEM((half, size, stop - start), jnp.float32),
            pltpu.VMEM((half, size, stop - start), jnp.bfloat16),
        ]
        held_columns = pltpu.VMEM((n // 2, rows, span), grad_out.dtype)
        params = pltpu.CompilerParams(vmem_limit_bytes=16 << 20)
        if left is None:
            *pair, left = pl.pallas_call(
                functools.partial(first_kernel, n, m, width),
                in_specs=[HBM] * 3 + [VMEM] * (n + 1),
                out_specs=[VMEM] * 3,
                out_shape=shapes + [pltpu.VMEM((2, rank, rows), jnp.bfloat16)],
                scratch_shapes=[
                    pltpu.VMEM(inputs.shape, inputs.dtype),
                    pltpu.VMEM(projection.shape, projection.dtype),
                    held_columns,
                    pltpu.SemaphoreType.DMA((n // 2 + 2,)),
                ],
                compiler_params=params,
                name="project",
            )(
                *placed(pltpu.HBM, inputs, projection, grad_out),
                *placed(pltpu.VMEM, inputs_too, *blocks[1:], grad_too),
            )
        else:
            pair = pl.pallas_call(
                functools.partial(next_kernel, n, m, width, chunk),
                in_specs=[HBM] + [VMEM] * 2,
                out_specs=[VMEM] * 2,
                out_shape=shapes,
                scratch_shapes=[held_columns, pltpu.SemaphoreType.DMA((n // 2,))],
                compiler_params=params,
                name="multiply",
            )(*placed(pltpu.HBM, grad_out), *placed(pltpu.VMEM, grad_too, left))
        sums += pair

    moment_t = lax.dynamic_slice_in_dim(moment.T, y * size, size)
    second_t = lax.dynamic_slice_in_dim(second.T, y * size, size)
    first_fix = 1.0 - 0.9**STEP
    second_fix = 1.0 - 0.999**STEP
    parts, fulls = [[], []], []
    for chunk, (start, stop) in enumerate(chunks_of(width)):
        steps = list(zip(*orders(n, m, chunk)))
        keep, send = sums[2 * chunk : 2 * chunk + 2]
        for s, both in enumerate(steps):
            got = lax.ppermute(send, AXES, pairs(n, m, both)).astype(jnp.float32)
            if s + 1 < len(steps):
                cut = keep.shape[0] // 2
                send = (keep[cut:] + got[cut:]).astype(jnp.bfloat16)
                keep = keep[:cut] + got[:cut]
            else:
                low_rank = (keep + got)[0]

        new_m = 0.9 * moment_t[:, start:stop] + 0.1 * low_rank
        new_s = 0.999 * second_t[:, start:stop] + 0.001 * (low_rank * low_rank)
        normalized = (new_m / first_fix / (jnp.sqrt(new_s / second_fix) + 1e-08)).astype(jnp.bfloat16)

        full = low_rank
        for k in range(bits_of(m)):
            got = lax.ppermute(full, "dp", [(w, w ^ (1 << k)) for w in range(m)])
            first = ((y >> k) & 1) == 0
            full = jnp.concatenate([jnp.where(first, full, got), jnp.where(first, got, full)], axis=0)

        held = normalized[None]
        for both in steps[:0:-1]:
            got = lax.ppermute(held, AXES, pairs(n, m, both))
            held = jnp.concatenate([held, got], axis=0)
        fulls.append(full)
        if stop == width:
            new_moment, new_second = pl.pallas_call(
                state_kernel,
                out_shape=[jax.ShapeDtypeStruct(moment.shape, jnp.float32)] * 2,
                compiler_params=pltpu.CompilerParams(vmem_limit_bytes=16 << 20),
                name="state",
            )(moment, second, *fulls)
        rest = lax.ppermute(held, AXES, pairs(n, m, steps[0]))
        if stop == width:
            rest, new_moment, new_second = lax.optimization_barrier((rest, new_moment, new_second))
        parts[0] += [held, rest]
        parts[1] += [lax.ppermute(held, "fsdp", partner), lax.ppermute(rest, "fsdp", partner)]

    relative = relative_ranks(projection, y, m)
    update = []
    for whose in ((0,), (1,)) if width % 128 == 0 else ((0, 1),):
        span = len(whose) * width
        sources = [part for other in whose for part in parts[other]]
        update = [
            pl.pallas_call(
                functools.partial(expand_kernel, n, m, width, whose),
                in_specs=[VMEM] * (1 + len(sources)) + [HBM] * len(update),
                out_specs=HBM,
                out_shape=jax.ShapeDtypeStruct((projection.shape[0], n * width), jnp.bfloat16),
                input_output_aliases={1 + len(sources): 0} if update else {},
                scratch_shapes=[
                    pltpu.VMEM((n // 2, projection.shape[0], span), jnp.bfloat16),
                    pltpu.SemaphoreType.DMA((n // 2,)),
                ],
                compiler_params=pltpu.CompilerParams(vmem_limit_bytes=16 << 20),
                name="expand",
            )(*placed(pltpu.VMEM, relative, *sources), *update)
        ]
    return (*update, new_moment, new_second)


def solution(mesh):
    in_specs = (
        P(AXES, None),
        P(AXES, None),
        P("fsdp", None),
        P("fsdp", None),
        P("fsdp", None),
    )
    out_specs = (P("fsdp", None), P("fsdp", None), P("fsdp", None))

    def body(*args):
        return local(mesh.shape["fsdp"], mesh.shape["dp"], *args)

    return jax.shard_map(body, mesh=mesh, in_specs=in_specs, out_specs=out_specs, check_vma=False)
```
